32 devices in a mesh: slab: 8 (over z, y), cross: 4 (over x, core).
Axes of the slice: x: 2, y: 2, z: 4, core: 2. Of those that a mesh axis runs over, the one named last changes fastest.
Arguments:
- a_tiles: bfloat16 [64, 7, 128, 128], P(('slab', 'cross')), may hold values from -0.1875 to 0.1875
- a_cols: int32 [64, 7], P(('slab', 'cross')), may hold values from 0 to 17, as said below
- over_tiles: bfloat16 [128, 128, 128], P(('slab', 'cross')), may hold values from -0.1875 to 0.1875
- over_rows: int32 [128], P(('slab', 'cross')), may hold values from 0 to 1
- over_cols: int32 [128], P(('slab', 'cross')), may hold values from 0 to 17
- p_tiles: bfloat16 [64, 3, 128, 128], P(('slab', 'cross')), may hold values from -0.8984375 to 0.8984375
- p_cols: int32 [64, 3], P(('slab', 'cross')), may hold values from 0 to 5, as said below
Outputs:
- coarse: float32 [2048, 1792], P(('slab', 'cross'))
The draws below stay inside these ranges and needn't reach their ends.
Inputs may be any that keep to these rules, and one draw needn't show every extreme that they name: `a_cols`: the 7 entries of a row are different. `p_cols`: the 3 entries of a row are different.
All inputs are finite; a program needn't handle non-finite values.
Results may differ from the reference program's by a relative error of at most 0.0063.
Values may be sent and summed in bfloat16 or wider, within the bound.
No kernel may reach another device: no remote copies, remote signals or barrier semaphores. Data moves between devices by JAX's collectives and lax.ppermute only.
A program may use at most 64 MiB of HBM per device.

```python
import jax
import jax.numpy as jnp
from jax import lax

TILE = 128
NB = 2
K = 7
OV = 4
KP = 3
CB = 2
NT = 64
OVT = 128
N_SLAB = 8
N_CROSS = 4


def distinct_columns(key, rows, span, count):
    scores = jax.random.randint(key, (rows, span), 0, 2 ** 20) * span + jnp.arange(span, dtype=jnp.int32)[None, :]
    order = jnp.argsort(scores, axis=1, stable=True)
    return order[:, :count].astype(jnp.int32)


def draw_a_cols(key, part):
    return distinct_columns(jax.random.fold_in(key, 11), NT, 9 * NB, K)


def draw_p_cols(key, part):
    return distinct_columns(jax.random.fold_in(key, 23), NT, 3 * CB, KP)


def plant(entries, key, low, top_value):
    longest = entries.shape.index(max(entries.shape))
    spots = []
    for shift in (0, 1):
        where = [jax.random.randint(jax.random.fold_in(key, axis), (), 0, length) for axis, length in enumerate(entries.shape)]
        where[longest] = (where[longest] + shift) % entries.shape[longest]
        spots.append(tuple(where))
    return entries.at[spots[0]].set(low).at[spots[1]].set(top_value)


def levels(key, dims, shards, low, top_value):
    def one(dim, blocks):
        heights = jax.random.uniform(jax.random.fold_in(jax.random.fold_in(key, 6), dim), (blocks,), jnp.float32, low / len(shards), top_value / len(shards))
        return jnp.repeat(jnp.exp(heights), dims[dim] // blocks).reshape((-1,) + (1,) * (len(dims) - dim - 1))

    gain = one(*shards[0])
    for cut in shards[1:]:
        gain = gain * one(*cut)
    return gain


def centred(stream_key, shape, scale, most, split=(), kind=jnp.bfloat16):
    entries = jax.random.normal(stream_key, shape, jnp.float32) * scale
    if len(split) > 0:
        entries = levels(stream_key, shape, split, -0.22, 0.18) * entries
    return jnp.clip(entries, min=-most, max=most).astype(kind)


def setup_inputs(seed: int = 0) -> dict:
    arg_keys = jax.random.split(jax.random.key(seed), 8)
    return {
        "a_tiles": centred(arg_keys[0], (NT, K, TILE, TILE), ((K + 1) * TILE) ** -0.5, 0.1875, ((0, 32),)),
        "a_cols": draw_a_cols(jax.random.fold_in(arg_keys[7], 71), 0),
        "over_tiles": centred(arg_keys[2], (OVT, TILE, TILE), ((K + 1) * TILE) ** -0.5, 0.1875, ((0, 32),)),
        "over_rows": plant(jax.random.randint(arg_keys[3], (OVT,), 0, NB), jax.random.fold_in(arg_keys[3], 1), 0, NB - 1).astype(jnp.int32),
        "over_cols": plant(jax.random.randint(arg_keys[4], (OVT,), 0, 9 * NB), jax.random.fold_in(arg_keys[4], 1), 0, (9 * NB) - 1).astype(jnp.int32),
        "p_tiles": centred(arg_keys[5], (NT, KP, TILE, TILE), 0.15, 0.8984375, ((0, 32),)),
        "p_cols": draw_p_cols(jax.random.fold_in(arg_keys[7], 71), 0),
    }


def dense_rows(p_tiles, p_cols):
    picks = (p_cols[:, :, None] == jnp.arange(3 * CB, dtype=jnp.int32)[None, None, :]).astype(jnp.float32)
    spread = jnp.einsum("nmq,nmab->naqb", picks, p_tiles.astype(jnp.float32))
    return spread.astype(jnp.bfloat16).reshape(p_tiles.shape[0], TILE, 3 * CB * TILE)


def device_part(a_tiles, a_cols, over_tiles, over_rows, over_cols, own_rows, extended):
    width = CB * TILE
    wide = 3 * width
    product = jnp.zeros((NB, TILE, 5 * width), jnp.float32)
    for k_index in range(K):
        rows = jnp.take(extended, a_cols[:, k_index], axis=0).astype(jnp.float32)
        piece = jnp.einsum("nab,nbq->naq", a_tiles[:, k_index].astype(jnp.float32), rows)
        offsets = a_cols[:, k_index] // (3 * NB)
        for shift_index in range(3):
            mask = (offsets == shift_index).astype(jnp.float32)[:, None, None]
            product = product.at[:, :, shift_index * width:shift_index * width + wide].add(mask * piece)
    rows = jnp.take(extended, over_cols, axis=0).astype(jnp.float32)
    piece = jnp.einsum("oab,obq->oaq", over_tiles.astype(jnp.float32), rows)
    row_pick = (over_rows[:, None] == jnp.arange(NB, dtype=jnp.int32)[None, :]).astype(jnp.float32)
    offsets = over_cols // (3 * NB)
    for shift_index in range(3):
        select = row_pick * (offsets == shift_index).astype(jnp.float32)[:, None]
        contrib = jnp.einsum("on,oaq->naq", select, piece)
        product = product.at[:, :, shift_index * width:shift_index * width + wide].add(contrib)
    product = product.astype(jnp.bfloat16).reshape(NB * TILE, 5 * width)
    return lax.dot_general(own_rows, product, (((0,), (0,)), ((), ())), preferred_element_type=jnp.float32)


def reference(a_tiles, a_cols, over_tiles, over_rows, over_cols, p_tiles, p_cols):
    width = CB * TILE
    dense_p = dense_rows(p_tiles, p_cols).reshape(N_SLAB, N_CROSS, NB, TILE, 3 * width)
    padded = jnp.pad(dense_p, ((1, 1), (1, 1), (0, 0), (0, 0), (0, 0)))
    a_all = a_tiles.reshape(N_SLAB, N_CROSS, NB, K, TILE, TILE)
    ac_all = a_cols.reshape(N_SLAB, N_CROSS, NB, K)
    ov_all = over_tiles.reshape(N_SLAB, N_CROSS, OV, TILE, TILE)
    orow_all = over_rows.reshape(N_SLAB, N_CROSS, OV)
    ocol_all = over_cols.reshape(N_SLAB, N_CROSS, OV)

    def one_slab(slab_index):
        window = lax.dynamic_slice_in_dim(padded, slab_index, 3, 0)
        own_slab = lax.dynamic_index_in_dim(dense_p, slab_index, 0, keepdims=False)
        total = jnp.zeros((3 * width, 5 * width), jnp.float32)
        for part_index in range(N_CROSS):
            extended = window[:, part_index:part_index + 3].reshape(9 * NB, TILE, 3 * width)
            own_rows = own_slab[part_index].reshape(NB * TILE, 3 * width)
            total = total + device_part(a_all[slab_index, part_index], ac_all[slab_index, part_index], ov_all[slab_index, part_index], orow_all[slab_index, part_index], ocol_all[slab_index, part_index], own_rows, extended)
        return total.reshape(3, width, 5 * width)

    parts = lax.map(one_slab, jnp.arange(N_SLAB, dtype=jnp.int32))
    zero_block = jnp.zeros((1, width, 5 * width), jnp.float32)
    lower = jnp.concatenate([zero_block, parts[:-1, 2]], axis=0)
    upper = jnp.concatenate([parts[1:, 0], zero_block], axis=0)
    coarse = jnp.zeros((N_SLAB, width, 7 * width), jnp.float32)
    coarse = coarse.at[:, :, 0:5 * width].add(lower)
    coarse = coarse.at[:, :, width:6 * width].add(parts[:, 1])
    coarse = coarse.at[:, :, 2 * width:7 * width].add(upper)
    return coarse.reshape(N_SLAB * width, 7 * width)
```

```python
import jax
import jax.numpy as jnp
from jax import lax
from jax.experimental import pallas as pl
from jax.experimental.pallas import tpu as pltpu
from jax.sharding import PartitionSpec as P

CB = 2
AXES = ("slab", "cross")
PAD = 16


def exchange(value, slabs, parts, move):
    pairs = []
    for s in range(slabs):
        for c in range(parts):
            t, d = move(s, c)
            pairs.append((s * parts + c, t * parts + d))
    return lax.ppermute(value, AXES, pairs)


def moves(slabs, parts):
    def odd(s):
        return (s - 1) % slabs if s % 2 == 0 else (s + 1) % slabs

    def across(c):
        d = c - 1 if c % 2 == 0 else c + 1
        return d if 0 <= d < parts else c

    return {
        "even": lambda s, c: (s ^ 1, c),
        "odd": lambda s, c: (odd(s), c),
        "pair": lambda s, c: (s, c ^ 1),
        "across": lambda s, c: (s, across(c)),
        "other": lambda s, c: (s, c ^ 2),
    }


def prepare_kernel(place, own, mate, own_cols, mate_cols, out):
    blocks, kp, tile = own.shape[0], own_cols.shape[1], own.shape[-1]
    half = tile // 2
    lower = place[0] == 0
    out[...] = jnp.zeros_like(out)
    for d, (source, cols) in enumerate(((own, own_cols), (mate, mate_cols))):
        for n in range(blocks):
            for m in range(kp):
                piece = source[n, m * tile : (m + 1) * tile, :]
                piece = jnp.where(lower, piece[:, :half], piece[:, half:])
                at = (d * blocks + n) * tile
                out[place[1 + cols[n, m]], :, at : at + tile] = piece.T


def product_kernel(info, a_cols, over_rows, over_cols, *refs):
    sources = refs[:9]
    a_tiles, over_tiles, out, ext, acc, cols_v, cols_s, sem = refs[9:]
    blocks, taps, tile = a_tiles.shape[0], a_tiles.shape[1], a_tiles.shape[-1]
    kp = ext.shape[-1] // tile
    for i, source in enumerate(sources):
        slot = info[2 * i]
        valid = info[2 * i + 1] == 1
        for n in range(blocks):
            row = source[n, kp * tile : kp * tile + PAD, :].astype(jnp.float32)
            cols_v[slot * blocks + n] = row[:8].astype(jnp.int32)
    copy = pltpu.make_async_copy(cols_v, cols_s, sem)
    copy.start()
    for i, source in enumerate(sources):
        slot = info[2 * i]
        valid = info[2 * i + 1] == 1
        for n in range(blocks):
            for m in range(kp):
                piece = source[n, m * tile : (m + 1) * tile, :]
                piece = jnp.where(valid, piece, jnp.zeros_like(piece))
                ext[slot * blocks + n, :, m * tile : (m + 1) * tile] = piece
    acc[...] = jnp.zeros_like(acc)
    copy.wait()

    def add(n, col, matrix):
        piece = jnp.dot(matrix, ext[col], preferred_element_type=jnp.float32)
        shift = (col // (3 * blocks)) * CB
        for m in range(kp):
            j = shift + cols_s[col, 0, m]
            acc[n, j] += piece[:, m * tile : (m + 1) * tile]

    for n in range(blocks):
        for k in range(taps):
            add(n, a_cols[n, k], a_tiles[n, k])
    for o in range(over_tiles.shape[0]):
        add(over_rows[o], over_cols[o], over_tiles[o])
    for n in range(blocks):
        for j in range(acc.shape[1]):
            out[n * tile : (n + 1) * tile, j * tile : (j + 1) * tile] = acc[n, j].astype(
                jnp.bfloat16
            )


def partial_kernel(left, own, mate, *outs):
    count, half = left.shape[0], left.shape[1]
    rows = own.shape[0]
    for i in range(count):
        block = left[i]
        total = jnp.dot(block[:, :rows], own[...], preferred_element_type=jnp.float32)
        total += jnp.dot(block[:, rows:], mate[...], preferred_element_type=jnp.float32)
        outs[i][...] = total.astype(outs[i].dtype)


def final_kernel(info, own, across, even, odd, out):
    width = (out.shape[1] - own.shape[1]) // 2
    span = own.shape[1]
    first = info[0] == 1
    odd_value = jnp.where(info[1] == 1, odd[...].astype(jnp.float32), 0.0)
    even_value = even[...].astype(jnp.float32)
    lower = jnp.where(first, odd_value, even_value)
    upper = jnp.where(first, even_value, odd_value)
    middle = own[...] + across[...].astype(jnp.float32)
    out[...] = jnp.zeros_like(out)
    out[:, :span] = lower
    out[:, width : width + span] += middle
    out[:, 2 * width : 2 * width + span] += upper


def vmem(count):
    return [pl.BlockSpec(memory_space=pltpu.VMEM)] * count


def smem(count):
    return [pl.BlockSpec(memory_space=pltpu.SMEM)] * count


def fast_body(slabs, parts, a_tiles, a_cols, over_tiles, over_rows, over_cols, p_tiles, p_cols):
    blocks, kp, tile = p_tiles.shape[0], p_tiles.shape[1], p_tiles.shape[-1]
    width = CB * tile
    span = blocks * tile
    half = tile // 2
    step = moves(slabs, parts)

    def send(value, name):
        return exchange(value, slabs, parts, step[name])

    slab = lax.axis_index("slab")
    part = lax.axis_index("cross")
    s_even = (slab % 2 == 0).astype(jnp.int32)
    c_even = (part % 2 == 0).astype(jnp.int32)
    odd_ok = jnp.where(s_even == 1, slab > 0, slab < slabs - 1).astype(jnp.int32)
    across_ok = jnp.where(c_even == 1, part > 0, part < parts - 1).astype(jnp.int32)
    r_even, r_odd = 2 * s_even, 2 - 2 * s_even
    u_pair, u_across = 2 * c_even, 2 - 2 * c_even

    cols = jnp.broadcast_to(
        jnp.pad(p_cols, ((0, 0), (0, tile - kp)))[:, None, :], (blocks, PAD, tile)
    ).astype(jnp.bfloat16)
    own = jnp.concatenate([p_tiles.reshape(blocks, kp * tile, tile), cols], axis=1)
    even = send(own, "even")
    odd = send(own, "odd")
    mate = send(own, "pair")
    own_x = send(own, "across")
    mate_cols = mate[:, kp * tile, :kp].astype(jnp.int32)
    even_p, odd_p = send(even, "pair"), send(odd, "pair")
    even_x, odd_x = send(even, "across"), send(odd, "across")

    side = part // 2
    q = jnp.arange(3 * CB, dtype=jnp.int32)
    block, owner = q // CB, q % CB
    here = owner == side
    place = jnp.where(
        block == 1,
        jnp.where(here, 5, 2),
        jnp.where((block == 2) == (s_even == 1), jnp.where(here, 4, 1), jnp.where(here, 3, 0)),
    )
    place = jnp.concatenate([(part % 2)[None], place]).astype(jnp.int32)
    left = pl.pallas_call(
        prepare_kernel,
        out_shape=jax.ShapeDtypeStruct((3 * CB, half, 2 * span), jnp.bfloat16),
        in_specs=smem(1) + vmem(2) + smem(2),
        out_specs=vmem(1)[0],
        cost_estimate=pl.CostEstimate(flops=0, bytes_accessed=1 << 20, transcendentals=0),
    )(place, own, mate, p_cols, mate_cols)

    one = jnp.int32(1)
    info = []
    for r, ok in ((one, one), (r_even, one), (r_odd, odd_ok)):
        for u, good in ((one, one), (u_pair, one), (u_across, across_ok)):
            info += [3 * r + u, ok * good]
    info = jnp.stack(info).astype(jnp.int32)
    product = pl.pallas_call(
        product_kernel,
        out_shape=jax.ShapeDtypeStruct((span, 5 * width), jnp.bfloat16),
        in_specs=smem(4) + vmem(11),
        out_specs=vmem(1)[0],
        scratch_shapes=[
            pltpu.VMEM((9 * blocks, tile, kp * tile), jnp.bfloat16),
            pltpu.VMEM((blocks, 5 * CB, tile, tile), jnp.float32),
            pltpu.VMEM((9 * blocks, 8, tile), jnp.int32),
            pltpu.SMEM((9 * blocks, 8, tile), jnp.int32),
            pltpu.SemaphoreType.DMA,
        ],
        cost_estimate=pl.CostEstimate(flops=1 << 29, bytes_accessed=1 << 22, transcendentals=0),
    )(
        info, a_cols, over_rows, over_cols,
        own, mate, own_x, even, even_p, even_x, odd, odd_p, odd_x,
        a_tiles, over_tiles,
    )
    product_mate = send(product, "pair")

    kinds = [jnp.bfloat16] * 3 + [jnp.float32] * 3
    x_odd, x_even, x_own, b_odd, b_even, b_own = pl.pallas_call(
        partial_kernel,
        out_shape=[jax.ShapeDtypeStruct((half, 5 * width), kind) for kind in kinds],
        in_specs=vmem(3),
        out_specs=vmem(6),
        cost_estimate=pl.CostEstimate(flops=1 << 29, bytes_accessed=1 << 22, transcendentals=0),
    )(left, product, product_mate)
    g_odd = send(x_odd, "other")
    g_even = send(x_even, "other")
    g_own = send(x_own, "other")
    s_odd = send((b_odd + g_odd.astype(jnp.float32)).astype(jnp.bfloat16), "odd")
    s_even_ = send((b_even + g_even.astype(jnp.float32)).astype(jnp.bfloat16), "even")
    return pl.pallas_call(
        final_kernel,
        out_shape=jax.ShapeDtypeStruct((half, 7 * width), jnp.float32),
        in_specs=smem(1) + vmem(4),
        out_specs=vmem(1)[0],
    )(jnp.stack([s_even, odd_ok]), b_own, g_own, s_even_, s_odd)


SPECS = (
    P(AXES, None, None, None),
    P(AXES, None),
    P(AXES, None, None),
    P(AXES),
    P(AXES),
    P(AXES, None, None, None),
    P(AXES, None),
)


def solution(mesh):
    slabs, parts = mesh.shape["slab"], mesh.shape["cross"]

    def body(*args):
        return fast_body(slabs, parts, *args)

    return jax.shard_map(
        body, mesh=mesh, in_specs=SPECS, out_specs=P(AXES, None), check_vma=False
    )
```

```python
import functools

import jax
import jax.numpy as jnp
from jax import lax
from jax.experimental import pallas as pl
from jax.experimental.pallas import tpu as pltpu
from jax.sharding import PartitionSpec as P

CB = 2
AXES = ("slab", "cross")
PAD = 16


def exchange(value, slabs, parts, move):
    pairs = []
    for s in range(slabs):
        for c in range(parts):
            t, d = move(s, c)
            pairs.append((s * parts + c, t * parts + d))
    return lax.ppermute(value, AXES, pairs)


def moves(slabs, parts):
    def odd(s):
        t = s - 1 if s % 2 == 0 else s + 1
        return t if 0 <= t < slabs else s

    def across(c):
        d = c - 1 if c % 2 == 0 else c + 1
        return d if 0 <= d < parts else c

    return {
        "even": lambda s, c: (s ^ 1, c),
        "odd": lambda s, c: (odd(s), c),
        "pair": lambda s, c: (s, c ^ 1),
        "across": lambda s, c: (s, across(c)),
        "other": lambda s, c: (s, c ^ 2),
    }


def pack_kernel(cols, tiles, out, sem):
    blocks, kp, tile = tiles.shape[0], tiles.shape[1], tiles.shape[-1]
    copies = []
    for n in range(blocks):
        for m in range(kp):
            copies.append(
                pltpu.make_async_copy(
                    tiles.at[n, m], out.at[n, m * tile : (m + 1) * tile], sem.at[n * kp + m]
                )
            )
    for copy in copies:
        copy.start()
    lane = lax.broadcasted_iota(jnp.int32, (PAD, tile), 1)
    for n in range(blocks):
        row = jnp.zeros((PAD, tile), jnp.int32)
        for m in range(kp):
            row = jnp.where(lane == m, cols[n, m], row)
        out[n, kp * tile :] = row.astype(jnp.float32).astype(jnp.bfloat16)
    for copy in copies:
        copy.wait()


def columns_of(sources, cols_v, cols_s, sem):
    for slot, source in sources:
        blocks, tile = source.shape[0], source.shape[-1]
        for n in range(blocks):
            row = source[n, source.shape[1] - PAD :].astype(jnp.float32)
            cols_v[slot * blocks + n] = row[:8].astype(jnp.int32)
    copy = pltpu.make_async_copy(cols_v, cols_s, sem)
    copy.start()
    return copy


def prepare_kernel(kp, own, mate, out, cols_v, cols_s, sem):
    blocks, tile = own.shape[0], own.shape[-1]
    half = tile // 2
    copy = columns_of(((0, own), (1, mate)), cols_v, cols_s, sem)
    part = lax.axis_index("cross")
    slab = lax.axis_index("slab")
    lower = lax.rem(part, 2) == 0
    side = lax.div(part, 2)
    even = lax.rem(slab, 2)
    out[...] = jnp.zeros_like(out)
    copy.wait()
    for d, source in enumerate((own, mate)):
        for n in range(blocks):
            for m in range(kp):
                piece = source[n, m * tile : (m + 1) * tile, :]
                piece = jnp.where(lower, piece[:, :half], piece[:, half:])
                at = (d * blocks + n) * tile
                q = cols_s[d * blocks + n, 0, m]
                block, owner = lax.div(q, CB), lax.rem(q, CB)
                to_even = (block == 2) == (even == 0)
                place = jnp.where(block == 1, 2, jnp.where(to_even, 1, 0))
                place += jnp.where(owner == side, 3, 0)
                out[place, :, at : at + tile] = piece.T


def product_kernel(slabs, parts, a_cols, over_rows, over_cols, *refs):
    sources = refs[:9]
    a_tiles, over_tiles, out, ext, acc, cols_v, cols_s, sem = refs[9:]
    blocks, taps, tile = a_tiles.shape[0], a_tiles.shape[1], a_tiles.shape[-1]
    kp = ext.shape[-1] // tile
    slab = lax.axis_index("slab")
    part = lax.axis_index("cross")
    r_even = 2 - 2 * lax.rem(slab, 2)
    u_pair = 2 - 2 * lax.rem(part, 2)
    r_odd, u_across = 2 - r_even, 2 - u_pair
    r_there = slab + r_odd - 1
    u_there = part + u_across - 1
    odd_ok = (r_there >= 0) & (r_there < slabs)
    across_ok = (u_there >= 0) & (u_there < parts)
    slots = [(3 * r + u) for r in (1, r_even, r_odd) for u in (1, u_pair, u_across)]
    valid = [
        None, None, across_ok, None, None, across_ok, odd_ok, odd_ok, odd_ok & across_ok
    ]
    copy = columns_of(list(zip(slots, sources)), cols_v, cols_s, sem)
    for slot, ok, source in zip(slots, valid, sources):
        for n in range(blocks):
            for m in range(kp):
                piece = source[n, m * tile : (m + 1) * tile, :]
                if ok is not None:
                    piece = jnp.where(ok, piece, jnp.zeros_like(piece))
                ext[slot * blocks + n, :, m * tile : (m + 1) * tile] = piece
    acc[...] = jnp.zeros_like(acc)
    copy.wait()

    def add(n, col, matrix):
        piece = jnp.dot(matrix, ext[col], preferred_element_type=jnp.float32)
        shift = (col // (3 * blocks)) * CB
        for m in range(kp):
            j = shift + cols_s[col, 0, m]
            acc[n, j] += piece[:, m * tile : (m + 1) * tile]

    for n in range(blocks):
        for k in range(taps):
            add(n, a_cols[n, k], a_tiles[n, k])
    for o in range(over_tiles.shape[0]):
        add(over_rows[o], over_cols[o], over_tiles[o])
    for n in range(blocks):
        for j in range(acc.shape[1]):
            out[n * tile : (n + 1) * tile, j * tile : (j + 1) * tile] = acc[n, j].astype(
                jnp.bfloat16
            )


def partial_kernel(left, own, mate, *outs):
    count, half = left.shape[0], left.shape[1]
    rows = own.shape[0]
    for i in range(count):
        block = left[i]
        total = jnp.dot(block[:, :rows], own[...], preferred_element_type=jnp.float32)
        total += jnp.dot(block[:, rows:], mate[...], preferred_element_type=jnp.float32)
        outs[i][...] = total.astype(outs[i].dtype)


def final_kernel(slabs, own, across, even, odd, out):
    width = (out.shape[1] - own.shape[1]) // 2
    span = own.shape[1]
    slab = lax.axis_index("slab")
    first = lax.rem(slab, 2) == 0
    there = jnp.where(first, slab - 1, slab + 1)
    ok = (there >= 0) & (there < slabs)
    odd_value = jnp.where(ok, odd[...].astype(jnp.float32), 0.0)
    even_value = even[...].astype(jnp.float32)
    lower = jnp.where(first, odd_value, even_value)
    upper = jnp.where(first, even_value, odd_value)
    middle = own[...] + across[...].astype(jnp.float32)
    out[...] = jnp.zeros_like(out)
    out[:, :span] = lower
    out[:, width : width + span] += middle
    out[:, 2 * width : 2 * width + span] += upper


def vmem(count):
    return [pl.BlockSpec(memory_space=pltpu.VMEM)] * count


def smem(count):
    return [pl.BlockSpec(memory_space=pltpu.SMEM)] * count


def cost(flops, size):
    return pl.CostEstimate(flops=flops, bytes_accessed=size, transcendentals=0)


def grant(mib):
    return pltpu.CompilerParams(vmem_limit_bytes=mib << 20)


def fast_body(slabs, parts, a_tiles, a_cols, over_tiles, over_rows, over_cols, p_tiles, p_cols):
    blocks, kp, tile = p_tiles.shape[0], p_tiles.shape[1], p_tiles.shape[-1]
    width = CB * tile
    span = blocks * tile
    half = tile // 2
    step = moves(slabs, parts)

    def send(value, name):
        return exchange(value, slabs, parts, step[name])

    def column_scratch(count):
        return [
            pltpu.VMEM((count * blocks, 8, tile), jnp.int32),
            pltpu.SMEM((count * blocks, 8, tile), jnp.int32),
            pltpu.SemaphoreType.DMA,
        ]

    own = pl.pallas_call(
        pack_kernel,
        out_shape=jax.ShapeDtypeStruct((blocks, kp * tile + PAD, tile), jnp.bfloat16),
        in_specs=smem(1) + [pl.BlockSpec(memory_space=pl.ANY)],
        out_specs=vmem(1)[0],
        scratch_shapes=[pltpu.SemaphoreType.DMA((blocks * kp,))],
        compiler_params=grant(2),
        cost_estimate=cost(0, 1 << 19),
        name="pack",
    )(p_cols, p_tiles)
    even = send(own, "even")
    odd = send(own, "odd")
    mate = send(own, "pair")
    own_x = send(own, "across")
    left = pl.pallas_call(
        functools.partial(prepare_kernel, kp),
        out_shape=jax.ShapeDtypeStruct((3 * CB, half, 2 * span), jnp.bfloat16),
        in_specs=vmem(2),
        out_specs=vmem(1)[0],
        scratch_shapes=column_scratch(2),
        compiler_params=grant(4),
        cost_estimate=cost(0, 1 << 20),
        name="prepare",
    )(own, mate)
    even, left = lax.optimization_barrier((even, left))
    even_p, odd_p = send(even, "pair"), send(odd, "pair")
    even_x, odd_x = send(even, "across"), send(odd, "across")
    product = pl.pallas_call(
        functools.partial(product_kernel, slabs, parts),
        out_shape=jax.ShapeDtypeStruct((span, 5 * width), jnp.bfloat16),
        in_specs=smem(3) + vmem(11),
        out_specs=vmem(1)[0],
        scratch_shapes=[
            pltpu.VMEM((9 * blocks, tile, kp * tile), jnp.bfloat16),
            pltpu.VMEM((blocks, 5 * CB, tile, tile), jnp.float32),
        ]
        + column_scratch(9),
        compiler_params=grant(12),
        cost_estimate=cost(1 << 29, 1 << 22),
        name="product",
    )(
        a_cols, over_rows, over_cols,
        own, mate, own_x, even, even_p, even_x, odd, odd_p, odd_x,
        a_tiles, over_tiles,
    )
    product_mate = send(product, "pair")

    kinds = [jnp.bfloat16] * 3 + [jnp.float32] * 3
    x_odd, x_even, x_own, b_odd, b_even, b_own = pl.pallas_call(
        partial_kernel,
        out_shape=[jax.ShapeDtypeStruct((half, 5 * width), kind) for kind in kinds],
        in_specs=vmem(3),
        out_specs=vmem(6),
        compiler_params=grant(8),
        cost_estimate=cost(1 << 29, 1 << 22),
        name="partial",
    )(left, product, product_mate)
    g_odd = send(x_odd, "other")
    g_even = send(x_even, "other")
    g_odd, x_own = lax.optimization_barrier((g_odd, x_own))
    s_odd = send((b_odd + g_odd.astype(jnp.float32)).astype(jnp.bfloat16), "odd")
    g_own = send(x_own, "other")
    s_even = send((b_even + g_even.astype(jnp.float32)).astype(jnp.bfloat16), "even")
    return pl.pallas_call(
        functools.partial(final_kernel, slabs),
        out_shape=jax.ShapeDtypeStruct((half, 7 * width), jnp.float32),
        in_specs=vmem(4),
        out_specs=vmem(1)[0],
        compiler_params=grant(4),
        name="final",
    )(b_own, g_own, s_even, s_odd)


SPECS = (
    P(AXES, None, None, None),
    P(AXES, None),
    P(AXES, None, None),
    P(AXES),
    P(AXES),
    P(AXES, None, None, None),
    P(AXES, None),
)


def solution(mesh):
    slabs, parts = mesh.shape["slab"], mesh.shape["cross"]

    def body(*args):
        return fast_body(slabs, parts, *args)

    return jax.shard_map(
        body, mesh=mesh, in_specs=SPECS, out_specs=P(AXES, None), check_vma=False
    )
```

```python
import functools

import jax
import jax.numpy as jnp
from jax import lax
from jax.experimental import pallas as pl
from jax.experimental.pallas import tpu as pltpu
from jax.sharding import PartitionSpec as P


CB = 2
AXES = ("slab", "cross")
PAD = 16
PHASES = ((0, 1, 2, 3, 4, 5, 6, 7), (8,))


def exchange(value, slabs, parts, move):
    pairs = []
    for s in range(slabs):
        for c in range(parts):
            t, d = move(s, c)
            pairs.append((s * parts + c, t * parts + d))
    return lax.ppermute(value, AXES, pairs)


def moves(slabs, parts):
    stand_in = 2 if slabs % 4 == 0 else 1

    def odd(s, c):
        t = s - 1 if s % 2 == 0 else s + 1
        return (t, c) if 0 <= t < slabs else (s, c ^ 1)

    def across(s, c):
        d = c - 1 if c % 2 == 0 else c + 1
        return (s, d) if 0 <= d < parts else (s ^ stand_in, c)

    return {
        "even": lambda s, c: (s ^ 1, c),
        "even_other": lambda s, c: (s ^ 1, c ^ 2),
        "odd": odd,
        "pair": lambda s, c: (s, c ^ 1),
        "across": across,
        "other": lambda s, c: (s, c ^ 2),
    }


def pack(p_tiles, p_cols):
    blocks, kp, tile = p_tiles.shape[0], p_tiles.shape[1], p_tiles.shape[-1]
    cols = jnp.pad(p_cols, ((0, 0), (0, tile - kp)))[:, None, :]
    cols = jnp.broadcast_to(cols, (blocks, PAD, tile)).astype(jnp.bfloat16)
    return jnp.concatenate([p_tiles.reshape(blocks, kp * tile, tile), cols], axis=1)


def columns_of(sources, cols_v, cols_s, sem):
    for slot, source in sources:
        blocks = source.shape[0]
        for n in range(blocks):
            row = source[n, source.shape[1] - PAD :].astype(jnp.float32)
            cols_v[pl.ds(slot * blocks + n, 1)] = row[:1].astype(jnp.int32)
    copy = pltpu.make_async_copy(cols_v, cols_s, sem)
    copy.start()
    return copy


def prepare_kernel(kp, own, mate, out, cols_v, cols_s, sem):
    blocks, tile = own.shape[0], own.shape[-1]
    half = tile // 2
    copy = columns_of(((0, own), (1, mate)), cols_v, cols_s, sem)
    part = lax.axis_index("cross")
    slab = lax.axis_index("slab")
    lower = lax.rem(part, 2) == 0
    side = lax.div(part, 2)
    even = lax.rem(slab, 2)
    out[...] = jnp.zeros_like(out)
    copy.wait()
    for d, source in enumerate((own, mate)):
        for n in range(blocks):
            for m in range(kp):
                piece = source[n, m * tile : (m + 1) * tile, :]
                piece = jnp.where(lower, piece[:, :half], piece[:, half:])
                at = (d * blocks + n) * tile
                q = cols_s[d * blocks + n, m]
                block, owner = lax.div(q, CB), lax.rem(q, CB)
                to_even = (block == 2) == (even == 0)
                place = jnp.where(block == 1, 2, jnp.where(to_even, 1, 0))
                place += jnp.where(owner == side, 3, 0)
                out[place, :, at : at + tile] = piece.T


def product_kernel(slabs, parts, phase, last, a_cols, over_rows, over_cols, *refs):
    sources, refs = refs[: len(phase)], refs[len(phase) :]
    a_tiles, over_tiles, refs = refs[0], refs[1], refs[2:]
    first = phase[0] == 0
    if not first:
        refs = refs[1:]
    if last:
        out, refs = refs[0], refs[1:]
    acc, ext, cols_v, cols_s, sem = refs
    blocks, taps, tile = a_tiles.shape[0], a_tiles.shape[1], a_tiles.shape[-1]
    kp = ext.shape[-1] // tile
    slab = lax.axis_index("slab")
    part = lax.axis_index("cross")
    r_even = 2 - 2 * lax.rem(slab, 2)
    u_pair = 2 - 2 * lax.rem(part, 2)
    r_odd, u_across = 2 - r_even, 2 - u_pair
    r_there = slab + r_odd - 1
    u_there = part + u_across - 1
    odd_ok = (r_there >= 0) & (r_there < slabs)
    across_ok = (u_there >= 0) & (u_there < parts)
    slots = [(3 * r + u) for r in (1, r_even, r_odd) for u in (1, u_pair, u_across)]
    valid = [
        None, None, across_ok, None, None, across_ok, odd_ok, odd_ok, odd_ok & across_ok
    ]
    copy = columns_of([(slots[i], x) for i, x in zip(phase, sources)], cols_v, cols_s, sem)
    for i, source in zip(phase, sources):
        for n in range(blocks):
            for m in range(kp):
                piece = source[n, m * tile : (m + 1) * tile, :]
                if first and valid[i] is not None:
                    piece = jnp.where(valid[i], piece, jnp.zeros_like(piece))
                ext[slots[i] * blocks + n, :, m * tile : (m + 1) * tile] = piece
    if first:
        for i in range(9):
            if i not in phase:
                for n in range(blocks):
                    ext[slots[i] * blocks + n] = jnp.zeros(ext.shape[1:], ext.dtype)
                    cols_v[pl.ds(slots[i] * blocks + n, 1)] = jnp.zeros((1, tile), cols_v.dtype)
        acc[...] = jnp.zeros_like(acc)
    copy.wait()

    def add(n, col, matrix):
        piece = jnp.dot(matrix[...], ext[col], preferred_element_type=jnp.float32)
        shift = (col // (3 * blocks)) * CB
        for m in range(kp):
            j = shift + cols_s[col, m]
            acc[n, j] += piece[:, m * tile : (m + 1) * tile]

    def visit(n, col, matrix):
        if first:
            add(n, col, matrix)
            return
        slot = lax.div(col, blocks)
        here = jnp.bool_(False)
        for i in phase:
            match = slot == slots[i]
            here = here | (match if valid[i] is None else match & valid[i])

        @pl.when(here)
        def _():
            add(n, col, matrix)

    for n in range(blocks):
        for k in range(taps):
            visit(n, a_cols[n, k], a_tiles.at[n, k])
    for o in range(over_tiles.shape[0]):
        visit(over_rows[o], over_cols[o], over_tiles.at[o])
    if last:
        for n in range(blocks):
            for j in range(acc.shape[1]):
                out[n * tile : (n + 1) * tile, j * tile : (j + 1) * tile] = acc[n, j].astype(
                    jnp.bfloat16
                )


def partial_kernel(left, own, mate, *outs):
    count = left.shape[0]
    rows = own.shape[0]
    for i in range(count):
        block = left[i]
        total = jnp.dot(block[:, :rows], own[...], preferred_element_type=jnp.float32)
        total += jnp.dot(block[:, rows:], mate[...], preferred_element_type=jnp.float32)
        outs[i][...] = total.astype(outs[i].dtype)


def final_kernel(slabs, own, across, even, even_x, odd, out):
    width = (out.shape[1] - own.shape[1]) // 2
    span = own.shape[1]
    slab = lax.axis_index("slab")
    first = lax.rem(slab, 2) == 0
    there = jnp.where(first, slab - 1, slab + 1)
    ok = (there >= 0) & (there < slabs)
    odd_value = jnp.where(ok, odd[...].astype(jnp.float32), 0.0)
    even_value = even[...].astype(jnp.float32) + even_x[...].astype(jnp.float32)
    lower = jnp.where(first, odd_value, even_value)
    upper = jnp.where(first, even_value, odd_value)
    middle = own[...] + across[...].astype(jnp.float32)
    out[...] = jnp.zeros_like(out)
    out[:, :span] = lower
    out[:, width : width + span] += middle
    out[:, 2 * width : 2 * width + span] += upper


def vmem(count):
    return [pl.BlockSpec(memory_space=pltpu.VMEM)] * count


def smem(count):
    return [pl.BlockSpec(memory_space=pltpu.SMEM)] * count


def cost(flops, size):
    return pl.CostEstimate(flops=flops, bytes_accessed=size, transcendentals=0)


def grant(mib):
    return pltpu.CompilerParams(vmem_limit_bytes=mib << 20)


def fast_body(slabs, parts, a_tiles, a_cols, over_tiles, over_rows, over_cols, p_tiles, p_cols):
    blocks, kp, tile = p_tiles.shape[0], p_tiles.shape[1], p_tiles.shape[-1]
    width = CB * tile
    span = blocks * tile
    half = tile // 2
    step = moves(slabs, parts)

    def send(value, name):
        return exchange(value, slabs, parts, step[name])

    def column_scratch(count):
        return [
            pltpu.VMEM((count * blocks, tile), jnp.int32),
            pltpu.SMEM((count * blocks, tile), jnp.int32),
            pltpu.SemaphoreType.DMA,
        ]

    own = pack(p_tiles, p_cols)
    even = send(own, "even")
    mate = send(own, "pair")
    own_x = send(own, "across")
    left = pl.pallas_call(
        functools.partial(prepare_kernel, kp),
        out_shape=jax.ShapeDtypeStruct((3 * CB, half, 2 * span), jnp.bfloat16),
        in_specs=vmem(2),
        out_specs=vmem(1)[0],
        scratch_shapes=column_scratch(2),
        compiler_params=grant(4),
        cost_estimate=cost(1 << 30, 1 << 24),
        name="prepare",
    )(own, mate)
    odd = send(own, "odd")
    even_x = send(even, "across")
    even_p = send(even, "pair")
    odd_x = send(odd, "across")
    odd_p = send(odd, "pair")
    sources = (own, mate, own_x, even, even_p, even_x, odd, odd_p, odd_x)
    sums = jax.ShapeDtypeStruct((blocks, 5 * CB, tile, tile), jnp.float32)
    rounded = jax.ShapeDtypeStruct((span, 5 * width), jnp.bfloat16)
    carried = ()
    for index, phase in enumerate(PHASES):
        last = index == len(PHASES) - 1
        results = pl.pallas_call(
            functools.partial(product_kernel, slabs, parts, phase, last),
            out_shape=(rounded, sums) if last else (sums,),
            in_specs=smem(3) + vmem(len(phase) + 2 + len(carried)),
            out_specs=(vmem(1)[0],) * (1 + last),
            scratch_shapes=[pltpu.VMEM((9 * blocks, tile, kp * tile), jnp.bfloat16)]
            + column_scratch(9),
            input_output_aliases={len(phase) + 5: int(last)} if carried else {},
            compiler_params=grant(8),
            cost_estimate=cost(1 << 30, 1 << 24),
            name="product",
        )(
            a_cols, over_rows, over_cols, *(sources[i] for i in phase), a_tiles, over_tiles,
            *carried,
        )
        carried = results[-1:]
    product = results[0]
    product_mate = send(product, "pair")

    kinds = [jnp.bfloat16] * 3 + [jnp.float32, jnp.bfloat16, jnp.float32]
    x_odd, x_even, x_own, b_odd, b_even, b_own = pl.pallas_call(
        partial_kernel,
        out_shape=[jax.ShapeDtypeStruct((half, 5 * width), kind) for kind in kinds],
        in_specs=vmem(3),
        out_specs=vmem(6),
        compiler_params=grant(8),
        cost_estimate=cost(1 << 29, 1 << 22),
        name="partial",
    )(left, product, product_mate)
    g_odd = send(x_odd, "other")
    g_even_x = send(x_even, "even_other")
    g_even = send(b_even, "even")
    g_own = send(x_own, "other")
    s_odd = send((b_odd + g_odd.astype(jnp.float32)).astype(jnp.bfloat16), "odd")
    return pl.pallas_call(
        functools.partial(final_kernel, slabs),
        out_shape=jax.ShapeDtypeStruct((half, 7 * width), jnp.float32),
        in_specs=vmem(5),
        out_specs=vmem(1)[0],
        compiler_params=grant(4),
        name="final",
    )(b_own, g_own, g_even, g_even_x, s_odd)


SPECS = (
    P(AXES, None, None, None),
    P(AXES, None),
    P(AXES, None, None),
    P(AXES),
    P(AXES),
    P(AXES, None, None, None),
    P(AXES, None),
)


def solution(mesh):
    slabs, parts = mesh.shape["slab"], mesh.shape["cross"]

    def body(*args):
        return fast_body(slabs, parts, *args)

    return jax.shard_map(
        body, mesh=mesh, in_specs=SPECS, out_specs=P(AXES, None), check_vma=False
    )
```

```python
import functools

import jax
import jax.numpy as jnp
from jax import lax
from jax.experimental import pallas as pl
from jax.experimental.pallas import tpu as pltpu
from jax.sharding import PartitionSpec as P


CB = 2
AXES = ("slab", "cross")
PAD = 16
LAST = 8


def exchange(value, slabs, parts, move):
    pairs = []
    for s in range(slabs):
        for c in range(parts):
            t, d = move(s, c)
            pairs.append((s * parts + c, t * parts + d))
    return lax.ppermute(value, AXES, pairs)


def moves(slabs, parts):
    stand_in = 2 if slabs % 4 == 0 else 1

    def odd(s, c):
        t = s - 1 if s % 2 == 0 else s + 1
        return (t, c) if 0 <= t < slabs else (s, c ^ 1)

    def across(s, c):
        d = c - 1 if c % 2 == 0 else c + 1
        return (s, d) if 0 <= d < parts else (s ^ stand_in, c)

    return {
        "even": lambda s, c: (s ^ 1, c),
        "even_other": lambda s, c: (s ^ 1, c ^ 2),
        "odd": odd,
        "pair": lambda s, c: (s, c ^ 1),
        "across": across,
        "other": lambda s, c: (s, c ^ 2),
    }


def pack(p_tiles, p_cols):
    blocks, kp, tile = p_tiles.shape[0], p_tiles.shape[1], p_tiles.shape[-1]
    cols = jnp.pad(p_cols, ((0, 0), (0, tile - kp)))[:, None, :]
    cols = jnp.broadcast_to(cols, (blocks, PAD, tile)).astype(jnp.bfloat16)
    return jnp.concatenate([p_tiles.reshape(blocks, kp * tile, tile), cols], axis=1)


def columns_of(sources, cols_v, cols_s, sem):
    for at, source in sources:
        for n in range(source.shape[0]):
            row = source[n, source.shape[1] - PAD :].astype(jnp.float32)
            cols_v[pl.ds(at + n, 1)] = row[:1].astype(jnp.int32)
    copy = pltpu.make_async_copy(cols_v, cols_s, sem)
    copy.start()
    return copy


def prepare_kernel(kp, own, mate, out, cols_v, cols_s, sem):
    blocks, tile = own.shape[0], own.shape[-1]
    half = tile // 2
    copy = columns_of(((0, own), (blocks, mate)), cols_v, cols_s, sem)
    part = lax.axis_index("cross")
    slab = lax.axis_index("slab")
    lower = lax.rem(part, 2) == 0
    side = lax.div(part, 2)
    even = lax.rem(slab, 2)
    out[...] = jnp.zeros_like(out)
    copy.wait()
    for d, source in enumerate((own, mate)):
        for n in range(blocks):
            for m in range(kp):
                piece = source[n, m * tile : (m + 1) * tile, :]
                piece = jnp.where(lower, piece[:, :half], piece[:, half:])
                at = (d * blocks + n) * tile
                q = cols_s[d * blocks + n, m]
                block, owner = lax.div(q, CB), lax.rem(q, CB)
                to_even = (block == 2) == (even == 0)
                place = jnp.where(block == 1, 2, jnp.where(to_even, 1, 0))
                place += jnp.where(owner == side, 3, 0)
                out[place, :, at : at + tile] = piece.T


class Place:
    def __init__(self, slabs, parts, blocks):
        slab, part = lax.axis_index("slab"), lax.axis_index("cross")
        r_even = 2 - 2 * lax.rem(slab, 2)
        u_pair = 2 - 2 * lax.rem(part, 2)
        r_odd, u_across = 2 - r_even, 2 - u_pair
        r_there, u_there = slab + r_odd - 1, part + u_across - 1
        odd_ok = (r_there >= 0) & (r_there < slabs)
        across_ok = (u_there >= 0) & (u_there < parts)
        self.shift = [r * CB for r in (1, r_even, r_odd) for _ in range(3)]
        self.first = [
            (3 * r + u) * blocks for r in (1, r_even, r_odd) for u in (1, u_pair, u_across)
        ]
        self.valid = [
            None, None, across_ok, None, None, across_ok, odd_ok, odd_ok, odd_ok & across_ok
        ]


def fetch(source, at, ok, ext):
    blocks, tile = source.shape[0], source.shape[-1]
    kp = ext.shape[-1] // tile
    for n in range(blocks):
        for m in range(kp):
            piece = source[n, m * tile : (m + 1) * tile, :]
            if ok is not None:
                piece = jnp.where(ok, piece, jnp.zeros_like(piece))
            ext[at + n, :, m * tile : (m + 1) * tile] = piece


def product_kernel(slabs, parts, a_cols, over_rows, over_cols, *refs):
    early = [i for i in range(9) if i != LAST]
    sources, refs = refs[:8], refs[8:]
    a_tiles, over_tiles, out, acc, ext, cols_v, cols_s, sem = refs
    blocks, taps, tile = a_tiles.shape[0], a_tiles.shape[1], a_tiles.shape[-1]
    kp = ext.shape[-1] // tile
    place = Place(slabs, parts, blocks)
    copy = columns_of(
        [(place.first[i], source) for i, source in zip(early, sources)], cols_v, cols_s, sem
    )
    for i, source in zip(early, sources):
        fetch(source, place.first[i], place.valid[i], ext)
    for n in range(blocks):
        ext[place.first[LAST] + n] = jnp.zeros(ext.shape[1:], ext.dtype)
        cols_v[pl.ds(place.first[LAST] + n, 1)] = jnp.zeros((1, tile), jnp.int32)
    acc[...] = jnp.zeros_like(acc)
    copy.wait()

    def add(n, col, matrix):
        piece = jnp.dot(matrix, ext[col], preferred_element_type=jnp.float32)
        shift = (col // (3 * blocks)) * CB
        for m in range(kp):
            acc[n, shift + cols_s[col, m]] += piece[:, m * tile : (m + 1) * tile]

    for n in range(blocks):
        for k in range(taps):
            add(n, a_cols[n, k], a_tiles[n, k])
    for o in range(over_tiles.shape[0]):
        add(over_rows[o], over_cols[o], over_tiles[o])
    for n in range(blocks):
        for j in range(acc.shape[1]):
            out[n * tile : (n + 1) * tile, j * tile : (j + 1) * tile] = acc[n, j].astype(
                jnp.bfloat16
            )


def last_kernel(slabs, parts, a_cols, over_rows, over_cols, source, a_tiles, over_tiles,
                acc_in, out_in, acc, out, ext, cols_v, cols_s, sem):
    blocks, taps, tile = a_tiles.shape[0], a_tiles.shape[1], a_tiles.shape[-1]
    kp = ext.shape[-1] // tile
    place = Place(slabs, parts, blocks)
    first, shift = place.first[LAST], place.shift[LAST]

    @pl.when(place.valid[LAST])
    def _():
        copy = columns_of([(0, source)], cols_v, cols_s, sem)
        fetch(source, 0, None, ext)
        copy.wait()

        def visit(n, col, matrix):
            row = col - first

            @pl.when((row >= 0) & (row < blocks))
            def _():
                piece = jnp.dot(matrix[...], ext[row], preferred_element_type=jnp.float32)
                at = pl.multiple_of(n * tile, tile)
                for m in range(kp):
                    j = shift + cols_s[row, m]
                    total = acc[n, j] + piece[:, m * tile : (m + 1) * tile]
                    acc[n, j] = total
                    to = pl.multiple_of(j * tile, tile)
                    out[pl.ds(at, tile), pl.ds(to, tile)] = total.astype(jnp.bfloat16)

        for n in range(blocks):
            for k in range(taps):
                visit(n, a_cols[n, k], a_tiles.at[n, k])
        for o in range(over_tiles.shape[0]):
            visit(over_rows[o], over_cols[o], over_tiles.at[o])


def partial_kernel(left, own, mate, *outs):
    count, half = left.shape[0], left.shape[1]
    rows = own.shape[0]
    stack = left[...].reshape(count * half, 2 * rows)
    total = jnp.dot(stack[:, :rows], own[...], preferred_element_type=jnp.float32)
    total += jnp.dot(stack[:, rows:], mate[...], preferred_element_type=jnp.float32)
    for i in range(count):
        outs[i][...] = total[i * half : (i + 1) * half].astype(outs[i].dtype)


def final_kernel(slabs, own, across, even, even_x, odd, out):
    width = (out.shape[1] - own.shape[1]) // 2
    span = own.shape[1]
    slab = lax.axis_index("slab")
    first = lax.rem(slab, 2) == 0
    there = jnp.where(first, slab - 1, slab + 1)
    ok = (there >= 0) & (there < slabs)
    odd_value = jnp.where(ok, odd[...].astype(jnp.float32), 0.0)
    even_value = even[...].astype(jnp.float32) + even_x[...].astype(jnp.float32)
    lower = jnp.where(first, odd_value, even_value)
    upper = jnp.where(first, even_value, odd_value)
    middle = own[...] + across[...].astype(jnp.float32)
    out[...] = jnp.zeros_like(out)
    out[:, :span] = lower
    out[:, width : width + span] += middle
    out[:, 2 * width : 2 * width + span] += upper


def vmem(count):
    return [pl.BlockSpec(memory_space=pltpu.VMEM)] * count


def smem(count):
    return [pl.BlockSpec(memory_space=pltpu.SMEM)] * count


def cost(flops, size):
    return pl.CostEstimate(flops=flops, bytes_accessed=size, transcendentals=0)


def grant(mib):
    return pltpu.CompilerParams(vmem_limit_bytes=mib << 20)


def fast_body(slabs, parts, a_tiles, a_cols, over_tiles, over_rows, over_cols, p_tiles, p_cols):
    blocks, kp, tile = p_tiles.shape[0], p_tiles.shape[1], p_tiles.shape[-1]
    width = CB * tile
    span = blocks * tile
    half = tile // 2
    step = moves(slabs, parts)

    def send(value, name):
        return exchange(value, slabs, parts, step[name])

    def column_scratch(count):
        return [
            pltpu.VMEM((count * blocks, tile), jnp.int32),
            pltpu.SMEM((count * blocks, tile), jnp.int32),
            pltpu.SemaphoreType.DMA,
        ]

    own = pack(p_tiles, p_cols)
    even = send(own, "even")
    mate = send(own, "pair")
    own_x = send(own, "across")
    left = pl.pallas_call(
        functools.partial(prepare_kernel, kp),
        out_shape=jax.ShapeDtypeStruct((3 * CB, half, 2 * span), jnp.bfloat16),
        in_specs=vmem(2),
        out_specs=vmem(1)[0],
        scratch_shapes=column_scratch(2),
        compiler_params=grant(4),
        cost_estimate=cost(1 << 30, 1 << 24),
        name="prepare",
    )(own, mate)
    odd = send(own, "odd")
    even_x = send(even, "across")
    even_p = send(even, "pair")
    odd_x = send(odd, "across")
    odd_p = send(odd, "pair")
    sources = (own, mate, own_x, even, even_p, even_x, odd, odd_p, odd_x)
    sums = jax.ShapeDtypeStruct((blocks, 5 * CB, tile, tile), jnp.float32)
    rounded = jax.ShapeDtypeStruct((span, 5 * width), jnp.bfloat16)
    product, acc = pl.pallas_call(
        functools.partial(product_kernel, slabs, parts),
        out_shape=(rounded, sums),
        in_specs=smem(3) + vmem(10),
        out_specs=vmem(2),
        scratch_shapes=[pltpu.VMEM((9 * blocks, tile, kp * tile), jnp.bfloat16)]
        + column_scratch(9),
        compiler_params=grant(8),
        cost_estimate=cost(1 << 30, 1 << 24),
        name="product",
    )(a_cols, over_rows, over_cols, *sources[:LAST], *sources[LAST + 1 :], a_tiles, over_tiles)
    acc, product = pl.pallas_call(
        functools.partial(last_kernel, slabs, parts),
        out_shape=(sums, rounded),
        in_specs=smem(3) + vmem(5),
        out_specs=vmem(2),
        scratch_shapes=[pltpu.VMEM((blocks, tile, kp * tile), jnp.bfloat16)]
        + column_scratch(1),
        input_output_aliases={6: 0, 7: 1},
        compiler_params=grant(4),
        cost_estimate=cost(1 << 30, 1 << 24),
        name="last",
    )(a_cols, over_rows, over_cols, sources[LAST], a_tiles, over_tiles, acc, product)
    product_mate = send(product, "pair")

    kinds = [jnp.bfloat16] * 3 + [jnp.float32, jnp.bfloat16, jnp.float32]
    x_odd, x_even, x_own, b_odd, b_even, b_own = pl.pallas_call(
        partial_kernel,
        out_shape=[jax.ShapeDtypeStruct((half, 5 * width), kind) for kind in kinds],
        in_specs=vmem(3),
        out_specs=vmem(6),
        compiler_params=grant(8),
        cost_estimate=cost(1 << 29, 1 << 22),
        name="partial",
    )(left, product, product_mate)
    g_odd = send(x_odd, "other")
    g_even_x = send(x_even, "even_other")
    g_even = send(b_even, "even")
    g_own = send(x_own, "other")
    s_odd = send((b_odd + g_odd.astype(jnp.float32)).astype(jnp.bfloat16), "odd")
    return pl.pallas_call(
        functools.partial(final_kernel, slabs),
        out_shape=jax.ShapeDtypeStruct((half, 7 * width), jnp.float32),
        in_specs=vmem(5),
        out_specs=vmem(1)[0],
        compiler_params=grant(4),
        name="final",
    )(b_own, g_own, g_even, g_even_x, s_odd)


SPECS = (
    P(AXES, None, None, None),
    P(AXES, None),
    P(AXES, None, None),
    P(AXES),
    P(AXES),
    P(AXES, None, None, None),
    P(AXES, None),
)


def solution(mesh):
    slabs, parts = mesh.shape["slab"], mesh.shape["cross"]

    def body(*args):
        return fast_body(slabs, parts, *args)

    return jax.shard_map(
        body, mesh=mesh, in_specs=SPECS, out_specs=P(AXES, None), check_vma=False
    )
```

```python
import functools

import jax
import jax.numpy as jnp
from jax import lax
from jax.experimental import pallas as pl
from jax.experimental.pallas import tpu as pltpu
from jax.sharding import PartitionSpec as P


CB = 2
AXES = ("slab", "cross")
LAST = 8


def exchange(value, slabs, parts, move):
    pairs = []
    for s in range(slabs):
        for c in range(parts):
            t, d = move(s, c)
            pairs.append((s * parts + c, t * parts + d))
    return lax.ppermute(value, AXES, pairs)


def moves(slabs, parts):
    stand_in = 2 if slabs % 4 == 0 else 1

    def odd(s, c):
        t = s - 1 if s % 2 == 0 else s + 1
        return (t, c) if 0 <= t < slabs else (s, c ^ 1)

    def across(s, c):
        d = c - 1 if c % 2 == 0 else c + 1
        return (s, d) if 0 <= d < parts else (s ^ stand_in, c)

    return {
        "even": lambda s, c: (s ^ 1, c),
        "even_other": lambda s, c: (s ^ 1, c ^ 2),
        "odd": odd,
        "pair": lambda s, c: (s, c ^ 1),
        "across": across,
        "across_self": lambda s, c: (s, across(s, c)[1]),
        "across_y": lambda s, c: across(s, c) if across(s, c)[0] == s else (s ^ 1, c),
        "across_x": lambda s, c: across(s, c) if across(s, c)[0] == s else (s, parts - 1 - c),
        "other": lambda s, c: (s, c ^ 2),
    }


def prepare_kernel(cols, own, mate, out):
    blocks, kp, tile = own.shape[0], own.shape[1], own.shape[-1]
    half = tile // 2
    part = lax.axis_index("cross")
    slab = lax.axis_index("slab")
    lower = lax.rem(part, 2) == 0
    side = lax.div(part, 2)
    even = lax.rem(slab, 2)
    out[...] = jnp.zeros_like(out)
    for d, source in enumerate((own, mate)):
        for n in range(blocks):
            for m in range(kp):
                piece = source[n, m]
                piece = jnp.where(lower, piece[:, :half], piece[:, half:])
                at = (d * blocks + n) * tile
                q = cols[d * blocks + n, m]
                block, owner = lax.div(q, CB), lax.rem(q, CB)
                to_even = (block == 2) == (even == 0)
                place = jnp.where(block == 1, 2, jnp.where(to_even, 1, 0))
                place += jnp.where(owner == side, 3, 0)
                out[place, :, at : at + tile] = piece.T


class Place:
    def __init__(self, slabs, parts, blocks):
        slab, part = lax.axis_index("slab"), lax.axis_index("cross")
        r_even = 2 - 2 * lax.rem(slab, 2)
        u_pair = 2 - 2 * lax.rem(part, 2)
        r_odd, u_across = 2 - r_even, 2 - u_pair
        r_there, u_there = slab + r_odd - 1, part + u_across - 1
        odd_ok = (r_there >= 0) & (r_there < slabs)
        across_ok = (u_there >= 0) & (u_there < parts)
        self.shift = [r * CB for r in (1, r_even, r_odd) for _ in range(3)]
        self.r_even, self.u_pair, self.blocks = r_even, u_pair, blocks
        self.first = [
            (3 * r + u) * blocks for r in (1, r_even, r_odd) for u in (1, u_pair, u_across)
        ]
        self.valid = [
            None, None, across_ok, None, None, across_ok, odd_ok, odd_ok, odd_ok & across_ok
        ]


    def columns(self, col):
        b = self.blocks
        r, rest = lax.div(col, 3 * b), lax.rem(col, 3 * b)
        u, n = lax.div(rest, b), lax.rem(rest, b)
        i = jnp.where(r == 1, 0, jnp.where(r == self.r_even, 1, 2))
        k = jnp.where(u == 1, 0, jnp.where(u == self.u_pair, 1, 2))
        return (3 * k + i) * b + n


def fetch(source, at, ok, ext):
    blocks, kp, tile = source.shape[0], source.shape[1], source.shape[-1]
    for n in range(blocks):
        for m in range(kp):
            piece = source[n, m]
            if ok is not None:
                piece = jnp.where(ok, piece, jnp.zeros_like(piece))
            ext[at + n, :, m * tile : (m + 1) * tile] = piece


def product_kernel(slabs, parts, cols, a_cols, over_rows, over_cols, *refs):
    early = [i for i in range(9) if i != LAST]
    sources, refs = refs[:8], refs[8:]
    a_tiles, over_tiles, out, acc, ext = refs
    blocks, taps, tile = a_tiles.shape[0], a_tiles.shape[1], a_tiles.shape[-1]
    kp = ext.shape[-1] // tile
    place = Place(slabs, parts, blocks)
    for i, source in zip(early, sources):
        fetch(source, place.first[i], place.valid[i], ext)
    for n in range(blocks):
        ext[place.first[LAST] + n] = jnp.zeros(ext.shape[1:], ext.dtype)
    acc[...] = jnp.zeros_like(acc)

    def add(n, col, matrix):
        piece = jnp.dot(matrix, ext[col], preferred_element_type=jnp.float32)
        shift = lax.div(col, 3 * blocks) * CB
        row = place.columns(col)
        for m in range(kp):
            acc[n, shift + cols[row, m]] += piece[:, m * tile : (m + 1) * tile]

    for n in range(blocks):
        for k in range(taps):
            add(n, a_cols[n, k], a_tiles[n, k])
    for o in range(over_tiles.shape[0]):
        add(over_rows[o], over_cols[o], over_tiles[o])
    for n in range(blocks):
        for j in range(acc.shape[1]):
            out[n * tile : (n + 1) * tile, j * tile : (j + 1) * tile] = acc[n, j].astype(
                jnp.bfloat16
            )


def last_kernel(slabs, parts, cols, a_cols, over_rows, over_cols, source, a_tiles, over_tiles,
                acc_in, out_in, acc, out, ext):
    blocks, taps, tile = a_tiles.shape[0], a_tiles.shape[1], a_tiles.shape[-1]
    kp = ext.shape[-1] // tile
    place = Place(slabs, parts, blocks)
    first, shift = place.first[LAST], place.shift[LAST]

    @pl.when(place.valid[LAST])
    def _():
        fetch(source, 0, None, ext)
        base = ((LAST % 3) * 3 + LAST // 3) * blocks

        def visit(n, col, matrix):
            row = col - first

            @pl.when((row >= 0) & (row < blocks))
            def _():
                piece = jnp.dot(matrix[...], ext[row], preferred_element_type=jnp.float32)
                at = pl.multiple_of(n * tile, tile)
                for m in range(kp):
                    j = shift + cols[base + row, m]
                    total = acc[n, j] + piece[:, m * tile : (m + 1) * tile]
                    acc[n, j] = total
                    to = pl.multiple_of(j * tile, tile)
                    out[pl.ds(at, tile), pl.ds(to, tile)] = total.astype(jnp.bfloat16)

        for n in range(blocks):
            for k in range(taps):
                visit(n, a_cols[n, k], a_tiles.at[n, k])
        for o in range(over_tiles.shape[0]):
            visit(over_rows[o], over_cols[o], over_tiles.at[o])


def partial_kernel(left, own, mate, *outs):
    count, half = left.shape[0], left.shape[1]
    rows = own.shape[0]
    stack = left[...].reshape(count * half, 2 * rows)
    total = jnp.dot(stack[:, :rows], own[...], preferred_element_type=jnp.float32)
    total += jnp.dot(stack[:, rows:], mate[...], preferred_element_type=jnp.float32)
    for i in range(count):
        outs[i][...] = total[i * half : (i + 1) * half].astype(outs[i].dtype)


def final_kernel(slabs, own, across, even, even_x, odd, out):
    width = (out.shape[1] - own.shape[1]) // 2
    span = own.shape[1]
    slab = lax.axis_index("slab")
    first = lax.rem(slab, 2) == 0
    there = jnp.where(first, slab - 1, slab + 1)
    ok = (there >= 0) & (there < slabs)
    odd_value = jnp.where(ok, odd[...].astype(jnp.float32), 0.0)
    even_value = even[...].astype(jnp.float32) + even_x[...].astype(jnp.float32)
    lower = jnp.where(first, odd_value, even_value)
    upper = jnp.where(first, even_value, odd_value)
    middle = own[...] + across[...].astype(jnp.float32)
    out[...] = jnp.zeros_like(out)
    out[:, :span] = lower
    out[:, width : width + span] += middle
    out[:, 2 * width : 2 * width + span] += upper


def vmem(count):
    return [pl.BlockSpec(memory_space=pltpu.VMEM)] * count


def smem(count):
    return [pl.BlockSpec(memory_space=pltpu.SMEM)] * count


def cost(flops, size):
    return pl.CostEstimate(flops=flops, bytes_accessed=size, transcendentals=0)


def grant(mib):
    return pltpu.CompilerParams(vmem_limit_bytes=mib << 20)


def fast_body(slabs, parts, a_tiles, a_cols, over_tiles, over_rows, over_cols, p_tiles, p_cols):
    blocks, kp, tile = p_tiles.shape[0], p_tiles.shape[1], p_tiles.shape[-1]
    width = CB * tile
    span = blocks * tile
    half = tile // 2
    step = moves(slabs, parts)

    def send(value, name):
        return exchange(value, slabs, parts, step[name])

    own = p_tiles
    cols_even = send(p_cols, "even")
    cols_odd = send(p_cols, "odd")
    near = jnp.concatenate([p_cols, cols_even, cols_odd])
    cols_pair = send(near, "pair")
    cols_across = send(near, "across")
    pair_cols = jnp.concatenate([p_cols, cols_pair[:blocks]])
    all_cols = jnp.concatenate([near, cols_pair, cols_across])
    even = send(own, "even")
    mate = send(own, "pair")
    own_x = send(own, "across_x")
    left = pl.pallas_call(
        prepare_kernel,
        out_shape=jax.ShapeDtypeStruct((3 * CB, half, 2 * span), jnp.bfloat16),
        in_specs=smem(1) + vmem(2),
        out_specs=vmem(1)[0],
        compiler_params=grant(4),
        cost_estimate=cost(1 << 30, 1 << 24),
        name="prepare",
    )(pair_cols, own, mate)
    odd = send(own, "odd")
    even_x = send(even, "across_self")
    even_p = send(even, "pair")
    odd_x = send(odd, "across")
    odd_p = send(odd, "pair")
    sources = (own, mate, own_x, even, even_p, even_x, odd, odd_p, odd_x)
    sums = jax.ShapeDtypeStruct((blocks, 5 * CB, tile, tile), jnp.float32)
    rounded = jax.ShapeDtypeStruct((span, 5 * width), jnp.bfloat16)
    product, acc = pl.pallas_call(
        functools.partial(product_kernel, slabs, parts),
        out_shape=(rounded, sums),
        in_specs=smem(4) + vmem(10),
        out_specs=vmem(2),
        scratch_shapes=[pltpu.VMEM((9 * blocks, tile, kp * tile), jnp.bfloat16)],
        compiler_params=grant(8),
        cost_estimate=cost(1 << 30, 1 << 24),
        name="product",
    )(all_cols, a_cols, over_rows, over_cols, *sources[:LAST], *sources[LAST + 1 :], a_tiles, over_tiles)
    acc, product = pl.pallas_call(
        functools.partial(last_kernel, slabs, parts),
        out_shape=(sums, rounded),
        in_specs=smem(4) + vmem(5),
        out_specs=vmem(2),
        scratch_shapes=[pltpu.VMEM((blocks, tile, kp * tile), jnp.bfloat16)],
        input_output_aliases={7: 0, 8: 1},
        compiler_params=grant(4),
        cost_estimate=cost(1 << 30, 1 << 24),
        name="last",
    )(all_cols, a_cols, over_rows, over_cols, sources[LAST], a_tiles, over_tiles, acc, product)
    product_mate = send(product, "pair")

    kinds = [jnp.bfloat16] * 3 + [jnp.float32, jnp.bfloat16, jnp.float32]
    x_odd, x_even, x_own, b_odd, b_even, b_own = pl.pallas_call(
        partial_kernel,
        out_shape=[jax.ShapeDtypeStruct((half, 5 * width), kind) for kind in kinds],
        in_specs=vmem(3),
        out_specs=vmem(6),
        compiler_params=grant(8),
        cost_estimate=cost(1 << 29, 1 << 22),
        name="partial",
    )(left, product, product_mate)
    g_odd = send(x_odd, "other")
    g_even_x = send(x_even, "even_other")
    g_even = send(b_even, "even")
    g_own = send(x_own, "other")
    s_odd = send((b_odd + g_odd.astype(jnp.float32)).astype(jnp.bfloat16), "odd")
    return pl.pallas_call(
        functools.partial(final_kernel, slabs),
        out_shape=jax.ShapeDtypeStruct((half, 7 * width), jnp.float32),
        in_specs=vmem(5),
        out_specs=vmem(1)[0],
        compiler_params=grant(4),
        name="final",
    )(b_own, g_own, g_even, g_even_x, s_odd)


SPECS = (
    P(AXES, None, None, None),
    P(AXES, None),
    P(AXES, None, None),
    P(AXES),
    P(AXES),
    P(AXES, None, None, None),
    P(AXES, None),
)


def solution(mesh):
    slabs, parts = mesh.shape["slab"], mesh.shape["cross"]

    def body(*args):
        return fast_body(slabs, parts, *args)

    return jax.shard_map(
        body, mesh=mesh, in_specs=SPECS, out_specs=P(AXES, None), check_vma=False
    )
```

```python
import functools

import jax
import jax.numpy as jnp
from jax import lax
from jax.experimental import pallas as pl
from jax.experimental.pallas import tpu as pltpu
from jax.sharding import PartitionSpec as P


CB = 2
AXES = ("slab", "cross")
PAD = 16
LAST = 8


def exchange(value, slabs, parts, move):
    pairs = []
    for s in range(slabs):
        for c in range(parts):
            t, d = move(s, c)
            pairs.append((s * parts + c, t * parts + d))
    return lax.ppermute(value, AXES, pairs)


def moves(slabs, parts):
    stand_in = 2 if slabs % 4 == 0 else 1

    def odd(s, c):
        t = s - 1 if s % 2 == 0 else s + 1
        return (t, c) if 0 <= t < slabs else (s, c ^ 1)

    def across(s, c):
        d = c - 1 if c % 2 == 0 else c + 1
        return (s, d) if 0 <= d < parts else (s ^ stand_in, c)

    return {
        "even": lambda s, c: (s ^ 1, c),
        "even_other": lambda s, c: (s ^ 1, c ^ 2),
        "odd": odd,
        "pair": lambda s, c: (s, c ^ 1),
        "across": across,
        "across_self": lambda s, c: (s, across(s, c)[1]),
        "across_y": lambda s, c: across(s, c) if across(s, c)[0] == s else (s ^ 1, c),
        "across_x": lambda s, c: across(s, c) if across(s, c)[0] == s else (s, parts - 1 - c),
        "other": lambda s, c: (s, c ^ 2),
    }


def pack(p_tiles, p_cols):
    blocks, kp, tile = p_tiles.shape[0], p_tiles.shape[1], p_tiles.shape[-1]
    cols = jnp.pad(p_cols, ((0, 0), (0, tile - kp)))[:, None, :]
    cols = jnp.broadcast_to(cols, (blocks, PAD, tile)).astype(jnp.bfloat16)
    return jnp.concatenate([p_tiles.reshape(blocks, kp * tile, tile), cols], axis=1)


def columns_of(sources, cols_v, cols_s, sem):
    for at, source in sources:
        for n in range(source.shape[0]):
            row = source[n, source.shape[1] - PAD :].astype(jnp.float32)
            cols_v[pl.ds(at + n, 1)] = row[:1].astype(jnp.int32)
    copy = pltpu.make_async_copy(cols_v, cols_s, sem)
    copy.start()
    return copy


def prepare_kernel(kp, own, mate, out, cols_v, cols_s, sem):
    blocks, tile = own.shape[0], own.shape[-1]
    half = tile // 2
    copy = columns_of(((0, own), (blocks, mate)), cols_v, cols_s, sem)
    part = lax.axis_index("cross")
    slab = lax.axis_index("slab")
    lower = lax.rem(part, 2) == 0
    side = lax.div(part, 2)
    even = lax.rem(slab, 2)
    out[...] = jnp.zeros_like(out)
    copy.wait()
    for d, source in enumerate((own, mate)):
        for n in range(blocks):
            for m in range(kp):
                piece = source[n, m * tile : (m + 1) * tile, :]
                piece = jnp.where(lower, piece[:, :half], piece[:, half:])
                at = (d * blocks + n) * tile
                q = cols_s[d * blocks + n, m]
                block, owner = lax.div(q, CB), lax.rem(q, CB)
                to_even = (block == 2) == (even == 0)
                place = jnp.where(block == 1, 2, jnp.where(to_even, 1, 0))
                place += jnp.where(owner == side, 3, 0)
                out[place, :, at : at + tile] = piece.T


class Place:
    def __init__(self, slabs, parts, blocks):
        slab, part = lax.axis_index("slab"), lax.axis_index("cross")
        r_even = 2 - 2 * lax.rem(slab, 2)
        u_pair = 2 - 2 * lax.rem(part, 2)
        r_odd, u_across = 2 - r_even, 2 - u_pair
        r_there, u_there = slab + r_odd - 1, part + u_across - 1
        odd_ok = (r_there >= 0) & (r_there < slabs)
        across_ok = (u_there >= 0) & (u_there < parts)
        self.shift = [r * CB for r in (1, r_even, r_odd) for _ in range(3)]
        self.first = [
            (3 * r + u) * blocks for r in (1, r_even, r_odd) for u in (1, u_pair, u_across)
        ]
        self.valid = [
            None, None, across_ok, None, None, across_ok, odd_ok, odd_ok, odd_ok & across_ok
        ]


def fetch(source, at, ok, ext):
    blocks, tile = source.shape[0], source.shape[-1]
    kp = ext.shape[-1] // tile
    for n in range(blocks):
        for m in range(kp):
            piece = source[n, m * tile : (m + 1) * tile, :]
            if ok is not None:
                piece = jnp.where(ok, piece, jnp.zeros_like(piece))
            ext[at + n, :, m * tile : (m + 1) * tile] = piece


def product_kernel(slabs, parts, a_cols, over_rows, over_cols, *refs):
    early = [i for i in range(9) if i != LAST]
    sources, refs = refs[:8], refs[8:]
    a_tiles, over_tiles, out, acc, ext, cols_v, cols_s, sem = refs
    blocks, taps, tile = a_tiles.shape[0], a_tiles.shape[1], a_tiles.shape[-1]
    kp = ext.shape[-1] // tile
    place = Place(slabs, parts, blocks)
    copy = columns_of(
        [(place.first[i], source) for i, source in zip(early, sources)], cols_v, cols_s, sem
    )
    for i, source in zip(early, sources):
        fetch(source, place.first[i], place.valid[i], ext)
    for n in range(blocks):
        ext[place.first[LAST] + n] = jnp.zeros(ext.shape[1:], ext.dtype)
        cols_v[pl.ds(place.first[LAST] + n, 1)] = jnp.zeros((1, tile), jnp.int32)
    acc[...] = jnp.zeros_like(acc)
    copy.wait()

    def add(n, col, matrix):
        piece = jnp.dot(matrix, ext[col], preferred_element_type=jnp.float32)
        shift = (col // (3 * blocks)) * CB
        for m in range(kp):
            acc[n, shift + cols_s[col, m]] += piece[:, m * tile : (m + 1) * tile]

    for n in range(blocks):
        for k in range(taps):
            add(n, a_cols[n, k], a_tiles[n, k])
    for o in range(over_tiles.shape[0]):
        add(over_rows[o], over_cols[o], over_tiles[o])
    for n in range(blocks):
        for j in range(acc.shape[1]):
            out[n * tile : (n + 1) * tile, j * tile : (j + 1) * tile] = acc[n, j].astype(
                jnp.bfloat16
            )


def last_kernel(slabs, parts, a_cols, over_rows, over_cols, source, a_tiles, over_tiles,
                acc_in, out_in, acc, out, ext, cols_s):
    blocks, taps, tile = a_tiles.shape[0], a_tiles.shape[1], a_tiles.shape[-1]
    kp = ext.shape[-1] // tile
    place = Place(slabs, parts, blocks)
    first, shift = place.first[LAST], place.shift[LAST]

    @pl.when(place.valid[LAST])
    def _():
        fetch(source, 0, None, ext)
        lane = lax.broadcasted_iota(jnp.int32, (1, tile), 1)
        lines = [source[n, source.shape[1] - PAD :].astype(jnp.float32)[:1] for n in range(blocks)]
        for n in range(blocks):
            for m in range(kp):
                value = jnp.sum(jnp.where(lane == m, lines[n], 0.0))
                cols_s[n, m] = value.astype(jnp.int32)

        def visit(n, col, matrix):
            row = col - first

            @pl.when((row >= 0) & (row < blocks))
            def _():
                piece = jnp.dot(matrix[...], ext[row], preferred_element_type=jnp.float32)
                at = pl.multiple_of(n * tile, tile)
                for m in range(kp):
                    j = shift + cols_s[row, m]
                    total = acc[n, j] + piece[:, m * tile : (m + 1) * tile]
                    acc[n, j] = total
                    to = pl.multiple_of(j * tile, tile)
                    out[pl.ds(at, tile), pl.ds(to, tile)] = total.astype(jnp.bfloat16)

        for n in range(blocks):
            for k in range(taps):
                visit(n, a_cols[n, k], a_tiles.at[n, k])
        for o in range(over_tiles.shape[0]):
            visit(over_rows[o], over_cols[o], over_tiles.at[o])


def partial_kernel(left, own, mate, *outs):
    count, half = left.shape[0], left.shape[1]
    rows = own.shape[0]
    stack = left[...].reshape(count * half, 2 * rows)
    total = jnp.dot(stack[:, :rows], own[...], preferred_element_type=jnp.float32)
    total += jnp.dot(stack[:, rows:], mate[...], preferred_element_type=jnp.float32)
    for i in range(count):
        outs[i][...] = total[i * half : (i + 1) * half].astype(outs[i].dtype)


def final_kernel(slabs, own, across, even, even_x, odd, out):
    width = (out.shape[1] - own.shape[1]) // 2
    span = own.shape[1]
    slab = lax.axis_index("slab")
    first = lax.rem(slab, 2) == 0
    there = jnp.where(first, slab - 1, slab + 1)
    ok = (there >= 0) & (there < slabs)
    odd_value = jnp.where(ok, odd[...].astype(jnp.float32), 0.0)
    even_value = even[...].astype(jnp.float32) + even_x[...].astype(jnp.float32)
    lower = jnp.where(first, odd_value, even_value)
    upper = jnp.where(first, even_value, odd_value)
    middle = own[...] + across[...].astype(jnp.float32)
    out[...] = jnp.zeros_like(out)
    out[:, :span] = lower
    out[:, width : width + span] += middle
    out[:, 2 * width : 2 * width + span] += upper


def vmem(count):
    return [pl.BlockSpec(memory_space=pltpu.VMEM)] * count


def smem(count):
    return [pl.BlockSpec(memory_space=pltpu.SMEM)] * count


def cost(flops, size):
    return pl.CostEstimate(flops=flops, bytes_accessed=size, transcendentals=0)


def grant(mib):
    return pltpu.CompilerParams(vmem_limit_bytes=mib << 20)


def fast_body(slabs, parts, a_tiles, a_cols, over_tiles, over_rows, over_cols, p_tiles, p_cols):
    blocks, kp, tile = p_tiles.shape[0], p_tiles.shape[1], p_tiles.shape[-1]
    width = CB * tile
    span = blocks * tile
    half = tile // 2
    step = moves(slabs, parts)

    def send(value, name):
        return exchange(value, slabs, parts, step[name])

    def column_scratch(count):
        return [
            pltpu.VMEM((count * blocks, tile), jnp.int32),
            pltpu.SMEM((count * blocks, tile), jnp.int32),
            pltpu.SemaphoreType.DMA,
        ]

    own = pack(p_tiles, p_cols)
    even = send(own, "even")
    mate = send(own, "pair")
    own_x = send(own, "across_x")
    left = pl.pallas_call(
        functools.partial(prepare_kernel, kp),
        out_shape=jax.ShapeDtypeStruct((3 * CB, half, 2 * span), jnp.bfloat16),
        in_specs=vmem(2),
        out_specs=vmem(1)[0],
        scratch_shapes=column_scratch(2),
        compiler_params=grant(4),
        cost_estimate=cost(1 << 30, 1 << 24),
        name="prepare",
    )(own, mate)
    odd = send(own, "odd")
    even_x = send(even, "across_self")
    even_p = send(even, "pair")
    odd_x = send(odd, "across")
    odd_p = send(odd, "pair")
    sources = (own, mate, own_x, even, even_p, even_x, odd, odd_p, odd_x)
    sums = jax.ShapeDtypeStruct((blocks, 5 * CB, tile, tile), jnp.float32)
    rounded = jax.ShapeDtypeStruct((span, 5 * width), jnp.bfloat16)
    product, acc = pl.pallas_call(
        functools.partial(product_kernel, slabs, parts),
        out_shape=(rounded, sums),
        in_specs=smem(3) + vmem(10),
        out_specs=vmem(2),
        scratch_shapes=[pltpu.VMEM((9 * blocks, tile, kp * tile), jnp.bfloat16)]
        + column_scratch(9),
        compiler_params=grant(8),
        cost_estimate=cost(1 << 30, 1 << 24),
        name="product",
    )(a_cols, over_rows, over_cols, *sources[:LAST], *sources[LAST + 1 :], a_tiles, over_tiles)
    acc, product = pl.pallas_call(
        functools.partial(last_kernel, slabs, parts),
        out_shape=(sums, rounded),
        in_specs=smem(3) + vmem(5),
        out_specs=vmem(2),
        scratch_shapes=[pltpu.VMEM((blocks, tile, kp * tile), jnp.bfloat16)]
        + [pltpu.SMEM((blocks, kp), jnp.int32)],
        input_output_aliases={6: 0, 7: 1},
        compiler_params=grant(4),
        cost_estimate=cost(1 << 30, 1 << 24),
        name="last",
    )(a_cols, over_rows, over_cols, sources[LAST], a_tiles, over_tiles, acc, product)
    product_mate = send(product, "pair")

    kinds = [jnp.bfloat16] * 3 + [jnp.float32, jnp.bfloat16, jnp.float32]
    x_odd, x_even, x_own, b_odd, b_even, b_own = pl.pallas_call(
        partial_kernel,
        out_shape=[jax.ShapeDtypeStruct((half, 5 * width), kind) for kind in kinds],
        in_specs=vmem(3),
        out_specs=vmem(6),
        compiler_params=grant(8),
        cost_estimate=cost(1 << 29, 1 << 22),
        name="partial",
    )(left, product, product_mate)
    g_odd = send(x_odd, "other")
    g_even_x = send(x_even, "even_other")
    g_even = send(b_even, "even")
    g_own = send(x_own, "other")
    s_odd = send((b_odd + g_odd.astype(jnp.float32)).astype(jnp.bfloat16), "odd")
    return pl.pallas_call(
        functools.partial(final_kernel, slabs),
        out_shape=jax.ShapeDtypeStruct((half, 7 * width), jnp.float32),
        in_specs=vmem(5),
        out_specs=vmem(1)[0],
        compiler_params=grant(4),
        name="final",
    )(b_own, g_own, g_even, g_even_x, s_odd)


SPECS = (
    P(AXES, None, None, None),
    P(AXES, None),
    P(AXES, None, None),
    P(AXES),
    P(AXES),
    P(AXES, None, None, None),
    P(AXES, None),
)


def solution(mesh):
    slabs, parts = mesh.shape["slab"], mesh.shape["cross"]

    def body(*args):
        return fast_body(slabs, parts, *args)

    return jax.shard_map(
        body, mesh=mesh, in_specs=SPECS, out_specs=P(AXES, None), check_vma=False
    )
```

```python
import functools

import jax
import jax.numpy as jnp
from jax import lax
from jax.experimental import pallas as pl
from jax.experimental.pallas import tpu as pltpu
from jax.sharding import PartitionSpec as P


CB = 2
AXES = ("slab", "cross")
PAD = 16
LAST = 8


def exchange(value, slabs, parts, move):
    pairs = []
    for s in range(slabs):
        for c in range(parts):
            t, d = move(s, c)
            pairs.append((s * parts + c, t * parts + d))
    return lax.ppermute(value, AXES, pairs)


def moves(slabs, parts):
    stand_in = 2 if slabs % 4 == 0 else 1

    def odd(s, c):
        t = s - 1 if s % 2 == 0 else s + 1
        return (t, c) if 0 <= t < slabs else (s, c ^ 1)

    def across(s, c):
        d = c - 1 if c % 2 == 0 else c + 1
        return (s, d) if 0 <= d < parts else (s ^ stand_in, c)

    return {
        "even": lambda s, c: (s ^ 1, c),
        "even_other": lambda s, c: (s ^ 1, c ^ 2),
        "odd": odd,
        "pair": lambda s, c: (s, c ^ 1),
        "across": across,
        "across_self": lambda s, c: (s, across(s, c)[1]),
        "across_y": lambda s, c: across(s, c) if across(s, c)[0] == s else (s ^ 1, c),
        "across_x": lambda s, c: across(s, c) if across(s, c)[0] == s else (s, parts - 1 - c),
        "other": lambda s, c: (s, c ^ 2),
    }


def pack(p_tiles, p_cols):
    blocks, kp, tile = p_tiles.shape[0], p_tiles.shape[1], p_tiles.shape[-1]
    tiles = jnp.pad(p_tiles.reshape(blocks, kp * tile, tile), ((0, 0), (0, PAD), (0, 0)))
    tiles, p_cols = lax.optimization_barrier((tiles, p_cols))
    cols = jnp.pad(p_cols, ((0, 0), (0, tile - kp)))[:, None, :]
    cols = jnp.broadcast_to(cols, (blocks, PAD, tile)).astype(jnp.bfloat16)
    return tiles.at[:, kp * tile :].set(cols)


def columns_of(sources, cols_v, cols_s, sem):
    for at, source in sources:
        for n in range(source.shape[0]):
            row = source[n, source.shape[1] - PAD :].astype(jnp.float32)
            cols_v[pl.ds(at + n, 1)] = row[:1].astype(jnp.int32)
    copy = pltpu.make_async_copy(cols_v, cols_s, sem)
    copy.start()
    return copy


def prepare_kernel(kp, own, mate, out, cols_v, cols_s, sem):
    blocks, tile = own.shape[0], own.shape[-1]
    half = tile // 2
    copy = columns_of(((0, own), (blocks, mate)), cols_v, cols_s, sem)
    part = lax.axis_index("cross")
    slab = lax.axis_index("slab")
    lower = lax.rem(part, 2) == 0
    side = lax.div(part, 2)
    even = lax.rem(slab, 2)
    out[...] = jnp.zeros_like(out)
    copy.wait()
    for d, source in enumerate((own, mate)):
        for n in range(blocks):
            for m in range(kp):
                piece = source[n, m * tile : (m + 1) * tile, :]
                piece = jnp.where(lower, piece[:, :half], piece[:, half:])
                at = (d * blocks + n) * tile
                q = cols_s[d * blocks + n, m]
                block, owner = lax.div(q, CB), lax.rem(q, CB)
                to_even = (block == 2) == (even == 0)
                place = jnp.where(block == 1, 2, jnp.where(to_even, 1, 0))
                place += jnp.where(owner == side, 3, 0)
                out[place, :, at : at + tile] = piece.T


class Place:
    def __init__(self, slabs, parts, blocks):
        slab, part = lax.axis_index("slab"), lax.axis_index("cross")
        r_even = 2 - 2 * lax.rem(slab, 2)
        u_pair = 2 - 2 * lax.rem(part, 2)
        r_odd, u_across = 2 - r_even, 2 - u_pair
        r_there, u_there = slab + r_odd - 1, part + u_across - 1
        odd_ok = (r_there >= 0) & (r_there < slabs)
        across_ok = (u_there >= 0) & (u_there < parts)
        self.shift = [r * CB for r in (1, r_even, r_odd) for _ in range(3)]
        self.first = [
            (3 * r + u) * blocks for r in (1, r_even, r_odd) for u in (1, u_pair, u_across)
        ]
        self.valid = [
            None, None, across_ok, None, None, across_ok, odd_ok, odd_ok, odd_ok & across_ok
        ]


def fetch(source, at, ok, ext):
    blocks, tile = source.shape[0], source.shape[-1]
    kp = ext.shape[-1] // tile
    for n in range(blocks):
        for m in range(kp):
            piece = source[n, m * tile : (m + 1) * tile, :]
            if ok is not None:
                piece = jnp.where(ok, piece, jnp.zeros_like(piece))
            ext[at + n, :, m * tile : (m + 1) * tile] = piece


def product_kernel(slabs, parts, a_cols, over_rows, over_cols, *refs):
    early = [i for i in range(9) if i != LAST]
    sources, refs = refs[:8], refs[8:]
    a_tiles, over_tiles, out, acc, ext, cols_v, cols_s, sem = refs
    blocks, taps, tile = a_tiles.shape[0], a_tiles.shape[1], a_tiles.shape[-1]
    kp = ext.shape[-1] // tile
    place = Place(slabs, parts, blocks)
    copy = columns_of(
        [(place.first[i], source) for i, source in zip(early, sources)], cols_v, cols_s, sem
    )
    for i, source in zip(early, sources):
        fetch(source, place.first[i], place.valid[i], ext)
    for n in range(blocks):
        ext[place.first[LAST] + n] = jnp.zeros(ext.shape[1:], ext.dtype)
        cols_v[pl.ds(place.first[LAST] + n, 1)] = jnp.zeros((1, tile), jnp.int32)
    acc[...] = jnp.zeros_like(acc)
    copy.wait()

    def add(n, col, matrix):
        piece = jnp.dot(matrix, ext[col], preferred_element_type=jnp.float32)
        shift = (col // (3 * blocks)) * CB
        for m in range(kp):
            acc[n, shift + cols_s[col, m]] += piece[:, m * tile : (m + 1) * tile]

    for n in range(blocks):
        for k in range(taps):
            add(n, a_cols[n, k], a_tiles[n, k])
    for o in range(over_tiles.shape[0]):
        add(over_rows[o], over_cols[o], over_tiles[o])
    for n in range(blocks):
        for j in range(acc.shape[1]):
            out[n * tile : (n + 1) * tile, j * tile : (j + 1) * tile] = acc[n, j].astype(
                jnp.bfloat16
            )


def last_kernel(slabs, parts, a_cols, over_rows, over_cols, source, a_tiles, over_tiles,
                acc_in, out_in, acc, out, ext, cols_s):
    blocks, taps, tile = a_tiles.shape[0], a_tiles.shape[1], a_tiles.shape[-1]
    kp = ext.shape[-1] // tile
    place = Place(slabs, parts, blocks)
    first, shift = place.first[LAST], place.shift[LAST]

    @pl.when(place.valid[LAST])
    def _():
        fetch(source, 0, None, ext)
        lane = lax.broadcasted_iota(jnp.int32, (1, tile), 1)
        lines = [source[n, source.shape[1] - PAD :].astype(jnp.float32)[:1] for n in range(blocks)]
        for n in range(blocks):
            for m in range(kp):
                value = jnp.sum(jnp.where(lane == m, lines[n], 0.0))
                cols_s[n, m] = value.astype(jnp.int32)

        def visit(n, col, matrix):
            row = col - first

            @pl.when((row >= 0) & (row < blocks))
            def _():
                piece = jnp.dot(matrix[...], ext[row], preferred_element_type=jnp.float32)
                at = pl.multiple_of(n * tile, tile)
                for m in range(kp):
                    j = shift + cols_s[row, m]
                    total = acc[n, j] + piece[:, m * tile : (m + 1) * tile]
                    acc[n, j] = total
                    to = pl.multiple_of(j * tile, tile)
                    out[pl.ds(at, tile), pl.ds(to, tile)] = total.astype(jnp.bfloat16)

        for n in range(blocks):
            for k in range(taps):
                visit(n, a_cols[n, k], a_tiles.at[n, k])
        for o in range(over_tiles.shape[0]):
            visit(over_rows[o], over_cols[o], over_tiles.at[o])


def own_part_kernel(left, own, total):
    stack = left[...].reshape(total.shape[0], left.shape[2])
    total[...] = jnp.dot(stack[:, : own.shape[0]], own[...], preferred_element_type=jnp.float32)


def partial_kernel(left, share, mate, *outs):
    count, half = left.shape[0], left.shape[1]
    stack = left[...].reshape(count * half, left.shape[2])
    total = share[...] + jnp.dot(
        stack[:, mate.shape[0] :], mate[...], preferred_element_type=jnp.float32
    )
    for i in range(count):
        outs[i][...] = total[i * half : (i + 1) * half].astype(outs[i].dtype)


def final_kernel(slabs, own, across, even, even_x, odd, out):
    width = (out.shape[1] - own.shape[1]) // 2
    span = own.shape[1]
    slab = lax.axis_index("slab")
    first = lax.rem(slab, 2) == 0
    there = jnp.where(first, slab - 1, slab + 1)
    ok = (there >= 0) & (there < slabs)
    odd_value = jnp.where(ok, odd[...].astype(jnp.float32), 0.0)
    even_value = even[...].astype(jnp.float32) + even_x[...].astype(jnp.float32)
    lower = jnp.where(first, odd_value, even_value)
    upper = jnp.where(first, even_value, odd_value)
    middle = own[...] + across[...].astype(jnp.float32)
    out[...] = jnp.zeros_like(out)
    out[:, :span] = lower
    out[:, width : width + span] += middle
    out[:, 2 * width : 2 * width + span] += upper


def vmem(count):
    return [pl.BlockSpec(memory_space=pltpu.VMEM)] * count


def smem(count):
    return [pl.BlockSpec(memory_space=pltpu.SMEM)] * count


def cost(flops, size):
    return pl.CostEstimate(flops=flops, bytes_accessed=size, transcendentals=0)


def grant(mib):
    return pltpu.CompilerParams(vmem_limit_bytes=mib << 20)


def fast_body(slabs, parts, a_tiles, a_cols, over_tiles, over_rows, over_cols, p_tiles, p_cols):
    blocks, kp, tile = p_tiles.shape[0], p_tiles.shape[1], p_tiles.shape[-1]
    width = CB * tile
    span = blocks * tile
    half = tile // 2
    step = moves(slabs, parts)

    def send(value, name):
        return exchange(value, slabs, parts, step[name])

    def column_scratch(count):
        return [
            pltpu.VMEM((count * blocks, tile), jnp.int32),
            pltpu.SMEM((count * blocks, tile), jnp.int32),
            pltpu.SemaphoreType.DMA,
        ]

    own = pack(p_tiles, p_cols)
    even = send(own, "even")
    mate = send(own, "pair")
    own_x = send(own, "across_x")
    left = pl.pallas_call(
        functools.partial(prepare_kernel, kp),
        out_shape=jax.ShapeDtypeStruct((3 * CB, half, 2 * span), jnp.bfloat16),
        in_specs=vmem(2),
        out_specs=vmem(1)[0],
        scratch_shapes=column_scratch(2),
        compiler_params=grant(4),
        cost_estimate=cost(1 << 30, 1 << 24),
        name="prepare",
    )(own, mate)
    odd = send(own, "odd")
    even_x = send(even, "across_self")
    even_p = send(even, "pair")
    odd_x = send(odd, "across")
    odd_p = send(odd, "pair")
    sources = (own, mate, own_x, even, even_p, even_x, odd, odd_p, odd_x)
    sums = jax.ShapeDtypeStruct((blocks, 5 * CB, tile, tile), jnp.float32)
    rounded = jax.ShapeDtypeStruct((span, 5 * width), jnp.bfloat16)
    product, acc = pl.pallas_call(
        functools.partial(product_kernel, slabs, parts),
        out_shape=(rounded, sums),
        in_specs=smem(3) + vmem(10),
        out_specs=vmem(2),
        scratch_shapes=[pltpu.VMEM((9 * blocks, tile, kp * tile), jnp.bfloat16)]
        + column_scratch(9),
        compiler_params=grant(8),
        cost_estimate=cost(1 << 30, 1 << 24),
        name="product",
    )(a_cols, over_rows, over_cols, *sources[:LAST], *sources[LAST + 1 :], a_tiles, over_tiles)
    acc, product = pl.pallas_call(
        functools.partial(last_kernel, slabs, parts),
        out_shape=(sums, rounded),
        in_specs=smem(3) + vmem(5),
        out_specs=vmem(2),
        scratch_shapes=[pltpu.VMEM((blocks, tile, kp * tile), jnp.bfloat16)]
        + [pltpu.SMEM((blocks, kp), jnp.int32)],
        input_output_aliases={6: 0, 7: 1},
        compiler_params=grant(4),
        cost_estimate=cost(1 << 30, 1 << 24),
        name="last",
    )(a_cols, over_rows, over_cols, sources[LAST], a_tiles, over_tiles, acc, product)
    product_mate = send(product, "pair")
    share = pl.pallas_call(
        own_part_kernel,
        out_shape=jax.ShapeDtypeStruct((3 * CB * half, 5 * width), jnp.float32),
        in_specs=vmem(2),
        out_specs=vmem(1)[0],
        compiler_params=grant(6),
        cost_estimate=cost(1 << 28, 1 << 21),
        name="own_part",
    )(left, product)

    kinds = [jnp.bfloat16] * 3 + [jnp.float32, jnp.bfloat16, jnp.float32]
    x_odd, x_even, x_own, b_odd, b_even, b_own = pl.pallas_call(
        partial_kernel,
        out_shape=[jax.ShapeDtypeStruct((half, 5 * width), kind) for kind in kinds],
        in_specs=vmem(3),
        out_specs=vmem(6),
        compiler_params=grant(8),
        cost_estimate=cost(1 << 29, 1 << 22),
        name="partial",
    )(left, share, product_mate)
    g_odd = send(x_odd, "other")
    g_even_x = send(x_even, "even_other")
    g_even = send(b_even, "even")
    g_own = send(x_own, "other")
    s_odd = send((b_odd + g_odd.astype(jnp.float32)).astype(jnp.bfloat16), "odd")
    return pl.pallas_call(
        functools.partial(final_kernel, slabs),
        out_shape=jax.ShapeDtypeStruct((half, 7 * width), jnp.float32),
        in_specs=vmem(5),
        out_specs=vmem(1)[0],
        compiler_params=grant(4),
        name="final",
    )(b_own, g_own, g_even, g_even_x, s_odd)


SPECS = (
    P(AXES, None, None, None),
    P(AXES, None),
    P(AXES, None, None),
    P(AXES),
    P(AXES),
    P(AXES, None, None, None),
    P(AXES, None),
)


def solution(mesh):
    slabs, parts = mesh.shape["slab"], mesh.shape["cross"]

    def body(*args):
        return fast_body(slabs, parts, *args)

    return jax.shard_map(
        body, mesh=mesh, in_specs=SPECS, out_specs=P(AXES, None), check_vma=False
    )
```
